512 devices in a mesh: energy: 32 (over y_lo, z, core), slab: 16 (over x, y_hi).
Axes of the slice: x: 4, y: 8 (y_hi: 4, y_lo: 2; y = y_hi * 2 + y_lo), z: 8, core: 2. Of those that a mesh axis runs over, the one named last changes fastest.
Arguments:
- green_old: bfloat16 [64, 16, 2, 256, 256], P('energy', 'slab'), may hold values from -1.25 to 1.25
- hopping: bfloat16 [16, 256, 256], P('slab'), may hold values from -0.0390625 to 0.0390625
- phonon_coupling: bfloat16 [16, 3, 256, 256], P('slab'), may hold values from -0.03125 to 0.03125
- band_offset: float32 [16, 256], P('slab'), may hold values from 0.35 to 0.55
- interface: float32 [16, 64, 64], P('slab'), may hold values from -0.09375 to 0.09375
- cell_counts: int32 [16], P('slab'), may hold values from 1 to 8, 80 in all
- contact_flags: int32 [16], P('slab'), may hold values 0 or 1
- phonon_shift: int32 [3], replicated, may hold values from 1 to 6, as said below
Outputs:
- green_new: float32 [64, 16, 2, 256, 256], P('energy', 'slab')
The draws below stay inside these ranges and needn't reach their ends.
Inputs may be any that keep to these rules, and one draw needn't show every extreme that they name: `phonon_shift`: mode k, counted from 0, has an offset from k * 2 + 1 to (k + 1) * 2; the last mode takes its top value.
All inputs are finite; a program needn't handle non-finite values. No bound on the sum of `cell_counts` or of `contact_flags` on one device may be relied on, other than what follows from the above.
Results may differ from the reference program's by a relative error of at most 0.0023.
Values may be sent and summed in bfloat16 or wider, within the bound.
No kernel may reach another device: no remote copies, remote signals or barrier semaphores. Data moves between devices by JAX's collectives and lax.ppermute only.
A program may use at most 64 MiB of HBM per device.

```python
import math
import jax
import jax.numpy as jnp
import numpy as np
from jax import lax

B = 256
FACE = 64
MODES = 3
NS_STEPS = 3
MAXCELL = 8
EPD = 2
ENERGIES = 64
SECTIONS = 16


def draw_phonon_shift(key, part):
    random_part = jax.random.randint(jax.random.fold_in(key, 11), (MODES,), 1, EPD + 1)
    topmost = jax.random.randint(jax.random.fold_in(key, 12), (), 0, MODES)
    modes_index = jnp.arange(MODES)
    random_part = jnp.where(modes_index == topmost, EPD, random_part)
    random_part = jnp.where(modes_index == MODES - 1, EPD, random_part)
    return (modes_index * EPD + random_part).astype(jnp.int32)


def with_ends(values, rng, smallest, high):
    longest = values.shape.index(max(values.shape))
    spots = []
    for shift in (0, 1):
        where = [jax.random.randint(jax.random.fold_in(rng, axis), (), 0, length) for axis, length in enumerate(values.shape)]
        where[longest] = (where[longest] + shift) % values.shape[longest]
        spots.append(tuple(where))
    return values.at[spots[0]].set(smallest).at[spots[1]].set(high)


def level_of(own_key, extent, split, least, top_value):
    level, own = 1.0, jax.random.fold_in(own_key, 6)
    for position, shards_of in split:
        draws = jnp.exp(jax.random.uniform(jax.random.fold_in(own, position), (shards_of,), jnp.float32, least / len(split), top_value / len(split)))
        level = level * jnp.repeat(draws, extent[position] // shards_of).reshape([-1 if axis == position else 1 for axis in range(len(extent))])
    return level


def split_up(count, total, most, slope):
    weights = [(1 << 20) // math.isqrt(grade ** slope) + 1 for grade in range(2, count + 1)]
    surplus, counts = total - most - (count - 1), [1] * (count - 1)
    while surplus > 0:
        free = [i for i in range(count - 1) if counts[i] < most]
        whole, left = sum([weights[i] for i in free]), surplus
        for i in free:
            addition = min(most - counts[i], max(1, left * weights[i] // whole), surplus)
            counts[i] = counts[i] + addition
            surplus = surplus - addition
    return np.array([most] + counts)


def uneven(rng, amount, total, reach, lean):
    if amount == 2:
        one = jax.random.randint(rng, (), max(1, total - reach), min(reach, total - 1) + 1)
        return jnp.stack([one, total - one])
    lengths = jnp.asarray(split_up(amount, total, reach, lean), jnp.int32)
    pairs = (amount - 1) // 2
    donor, taker = lengths[1:1 + 2 * pairs:2], lengths[2:2 + 2 * pairs:2]
    margin = jnp.minimum(donor - 1, reach - taker)
    passed = jax.random.randint(jax.random.fold_in(rng, 1), (pairs,), 0, 1 << 20) % (margin + 1)
    lengths = lengths.at[1:1 + 2 * pairs:2].set(donor - passed).at[2:2 + 2 * pairs:2].set(taker + passed)
    return lengths[jax.random.permutation(jax.random.fold_in(rng, 2), amount)]


def centred(key, shape, deviation, limit, shards=(), held_as=jnp.bfloat16):
    result = jax.random.normal(key, shape, jnp.float32) * deviation
    if len(shards) > 0:
        result = level_of(key, shape, shards, -0.22, 0.18) * result
    return jnp.clip(result, min=-limit, max=limit).astype(held_as)


def setup_inputs(seed: int = 0) -> dict:
    arg_keys = jax.random.split(jax.random.key(seed), 9)
    return {
        "green_old": centred(arg_keys[0], (ENERGIES, SECTIONS, 2, B, B), 0.5, 1.25, ((0, 32), (1, 16))),
        "hopping": centred(arg_keys[1], (SECTIONS, B, B), (100 * B) ** -0.5, 0.0390625, ((0, 16),)),
        "phonon_coupling": centred(arg_keys[2], (SECTIONS, MODES, B, B), (160 * B) ** -0.5, 0.03125, ((0, 16),)),
        "band_offset": jnp.clip(0.35 + 0.20000002 * jax.random.uniform(arg_keys[3], (SECTIONS, B), jnp.float32) ** level_of(arg_keys[3], (SECTIONS, B), ((0, 16),), -0.2, 0.2), 0.35, 0.55),
        "interface": centred(arg_keys[4], (SECTIONS, FACE, FACE), (72 * FACE) ** -0.5, 0.09375, ((0, 16),), jnp.float32),
        "cell_counts": uneven(arg_keys[5], SECTIONS, 5 * SECTIONS, MAXCELL, 0).astype(jnp.int32),
        "contact_flags": with_ends((jax.random.randint(arg_keys[6], (SECTIONS,), 0, 3) < 1).astype(jnp.int32), jax.random.fold_in(arg_keys[6], 1), 0, 1),
        "phonon_shift": draw_phonon_shift(jax.random.fold_in(arg_keys[8], 71), 0),
    }


broadening = 0.05
contact_width = 0.15
damping = 0.75
level_start = -0.05
level_range = 0.1
highest = lax.Precision.HIGHEST


def complex_product(left, right):
    real_real = jnp.einsum('sij,sjk->sik', left[:, 0], right[:, 0], precision=highest)
    imag_imag = jnp.einsum('sij,sjk->sik', left[:, 1], right[:, 1], precision=highest)
    real_imag = jnp.einsum('sij,sjk->sik', left[:, 0], right[:, 1], precision=highest)
    imag_real = jnp.einsum('sij,sjk->sik', left[:, 1], right[:, 0], precision=highest)
    return jnp.stack((real_real - imag_imag, real_imag + imag_real), 1)


def reference(green_old, hopping, phonon_coupling, band_offset, interface, cell_counts, contact_flags, phonon_shift):
    energies = green_old.shape[0]
    orbitals = green_old.shape[3]
    face = interface.shape[1]
    symmetric = 0.5 * (hopping.astype(jnp.float32) + jnp.swapaxes(hopping, 1, 2).astype(jnp.float32))
    weight = cell_counts.astype(jnp.float32) / MAXCELL
    width = broadening + contact_width * contact_flags.astype(jnp.float32)
    eye_big = jnp.eye(orbitals, dtype=jnp.float32)
    coupling = phonon_coupling.astype(jnp.float32)
    zero_face = jnp.zeros((1, 2, face, face), jnp.float32)
    zero_coupling = jnp.zeros((1, face, face), jnp.float32)
    left_coupling = jnp.concatenate((zero_coupling, interface[:-1]), 0)

    def one_energy(energy_index):
        total = jnp.zeros(green_old.shape[1:], jnp.float32)
        for mode in range(MODES):
            lower = jnp.mod(energy_index - phonon_shift[mode], energies).astype(jnp.int32)
            upper = jnp.mod(energy_index + phonon_shift[mode], energies).astype(jnp.int32)
            first = lax.dynamic_index_in_dim(green_old, lower, 0, False).astype(jnp.float32)
            second = lax.dynamic_index_in_dim(green_old, upper, 0, False).astype(jnp.float32)
            pair = (first + second).astype(jnp.bfloat16)
            half = jnp.einsum('sij,scjl->scil', coupling[:, mode], pair.astype(jnp.float32), precision=highest)
            half = half.astype(jnp.bfloat16)
            total = total + jnp.einsum('scil,sml->scim', half.astype(jnp.float32), coupling[:, mode], precision=highest)
        sigma = total * weight[:, None, None, None]
        level = level_start + level_range * energy_index.astype(jnp.float32) / energies
        real_diag = level + band_offset
        imag_diag = jnp.broadcast_to(width[:, None], real_diag.shape)
        base = jnp.stack((eye_big * real_diag[:, None, :] - symmetric, eye_big * imag_diag[:, None, :]), 1) - sigma
        denom = real_diag * real_diag + imag_diag * imag_diag
        diagonal = jnp.stack((real_diag / denom, -imag_diag / denom), 1)
        iterate = eye_big * diagonal[:, :, None, :]
        for step in range(NS_STEPS):
            left_face = iterate[:, :, :face, :face]
            right_face = iterate[:, :, orbitals - face:, orbitals - face:]
            from_left = jnp.concatenate((zero_face, right_face[:-1]), 0)
            from_right = jnp.concatenate((left_face[1:], zero_face), 0)
            inner = jnp.einsum('sba,scbd->scad', left_coupling, from_left, precision=highest)
            inner = jnp.einsum('scad,sde->scae', inner, left_coupling, precision=highest)
            outer = jnp.einsum('sab,scbd->scad', interface, from_right, precision=highest)
            outer = jnp.einsum('scad,sed->scae', outer, interface, precision=highest)
            system = base.at[:, :, :face, :face].add(-inner)
            system = system.at[:, :, orbitals - face:, orbitals - face:].add(-outer)
            residual = -complex_product(system, iterate)
            residual = residual.at[:, 0].add(eye_big)
            iterate = iterate + damping * complex_product(iterate, residual)
        return iterate

    return lax.map(one_energy, jnp.arange(energies, dtype=jnp.int32))
```

```python
import jax
import jax.numpy as jnp
from jax import lax
from jax.experimental import pallas as pl
from jax.experimental.pallas import tpu as pltpu
from jax.sharding import PartitionSpec as P

MAXCELL = 8

broadening = 0.05
contact_width = 0.15
damping = 0.75
level_start = -0.05
level_range = 0.1

B = 256
F = 64
F32 = jnp.float32
BF16 = jnp.bfloat16
VMEM = pl.BlockSpec(memory_space=pltpu.VMEM)
SMEM = pl.BlockSpec(memory_space=pltpu.SMEM)
highest = lax.Precision.HIGHEST


def mm(left, right):
    return jnp.dot(left, right, preferred_element_type=F32)


def mm_nt(left, right):
    return lax.dot_general(left, right, (((1,), (1,)), ((), ())), preferred_element_type=F32)


def exact(left, right):
    return jnp.dot(left, right, precision=highest, preferred_element_type=F32)


def halves(value):
    high = value.astype(BF16)
    return high, (value - high.astype(F32)).astype(BF16)


def mm3(left, right):
    return mm(left[0], right[0]) + (mm(left[0], right[1]) + mm(left[1], right[0]))


def complex_mm(left, right):
    real = mm3(left[0], right[0]) - mm3(left[1], right[1])
    imag = mm3(left[0], right[1]) + mm3(left[1], right[0])
    return real, imag


def levels():
    first = lax.axis_index("energy") * 2
    energies = 2 * lax.axis_size("energy")
    return [level_start + level_range * (first + e).astype(F32) / energies for e in range(2)]


def inverse(real, width):
    denom = real * real + width * width
    return real / denom, -width / denom


def call(kernel, outs, n_smem, n_vmem, flops, scratch=(), **kw):
    return pl.pallas_call(
        kernel,
        out_shape=[jax.ShapeDtypeStruct(shape, dtype) for shape, dtype in outs],
        in_specs=[SMEM] * n_smem + [VMEM] * n_vmem,
        out_specs=[VMEM] * len(outs),
        scratch_shapes=list(scratch),
        cost_estimate=pl.CostEstimate(flops=flops, bytes_accessed=1 << 20, transcendentals=0),
        compiler_params=pltpu.CompilerParams(vmem_limit_bytes=32 << 20),
        **kw,
    )


def pack_kernel(contact, interface, offset, out):
    out[...] = jnp.zeros_like(out)
    out[0:F, 0:F] = interface[...]
    out[F : F + 1, :] = offset[:, 0:128]
    out[F + 1 : F + 2, :] = offset[:, 128:256]
    out[F + 2 : F + 3, :] = jnp.full((1, 128), contact[0].astype(F32))


def pick(odd, when_even, when_odd):
    return jnp.where(odd, when_odd, when_even)


def prepare_kernel(hopping, own, recv_e, recv_o, base, packed0, self0, rows, cols, mats):
    slab = lax.axis_index("slab")
    odd = slab % 2 == 1
    before = pick(odd, recv_o[...], recv_e[...])
    after = pick(odd, recv_e[...], recv_o[...])
    mine = own[...]
    has_after = jnp.where(slab < lax.axis_size("slab") - 1, 1.0, 0.0)
    level = levels()
    zero = jnp.zeros((F, 128), F32)

    def width_of(pack):
        return broadening + contact_width * pack[F + 2 : F + 3, :]

    def column(row):
        return jnp.broadcast_to(row, (128, 128)).T

    def down(matrix):
        return jnp.concatenate((matrix, zero), 0)

    def up(matrix):
        return jnp.concatenate((zero, matrix), 0)

    v_own, v_before = mine[0:F], before[0:F]
    mats[0] = up(v_own).T.astype(BF16)
    mats[1] = up(v_own).astype(BF16)
    mats[2] = down(v_before).astype(BF16)
    mats[3] = down(v_before).T.astype(BF16)

    def inner_of(pack, e):
        v = pack[0:F]
        w = width_of(pack)[:, 0:1]
        real, imag = inverse(level[e] + column(pack[F + 1 : F + 2])[F:128], w)
        return [exact(down(v * x).T, down(v))[0:F] for x in (real, imag)]

    def outer_of(v, pack, e):
        real, imag = inverse(level[e] + pack[F : F + 1], width_of(pack))
        return [exact(v * x, down(v).T) for x in (real, imag)]

    sym = hopping[...].astype(F32)
    sym = 0.5 * (sym + sym.T)
    left_row, right_row = mine[F : F + 1], mine[F + 1 : F + 2]
    left_col, right_col = column(left_row), column(right_row)
    width = width_of(mine)
    for e in range(2):
        inner = inner_of(before, e)
        outer = [x * has_after for x in outer_of(v_own, after, e)]
        to_right = inner_of(mine, e)
        to_left = outer_of(v_before, mine, e)
        base[e, 0] = sym
        base[e, 1] = jnp.zeros((B, B), F32)
        for c in range(2):
            base[e, c, 0:F, 0:128] += inner[c]
            base[e, c, B - F : B, 128:256] += pltpu.roll(outer[c], F, 1)
        packed0[e, 0] = inner[0] + pltpu.roll(inner[1], F, 1)
        packed0[e, 1] = outer[0] + pltpu.roll(outer[1], F, 1)
        self0[e, 0] = to_right[0] + pltpu.roll(to_right[1], F, 1)
        self0[e, 1] = to_left[0] + pltpu.roll(to_left[1], F, 1)
        for part, (row, col) in enumerate(((left_row, left_col), (right_row, right_col))):
            lanes = slice(128 * part, 128 * part + 128)
            real, imag = inverse(level[e] + row, width)
            rows[2 * e : 2 * e + 1, lanes] = real
            rows[2 * e + 1 : 2 * e + 2, lanes] = imag
            real, imag = inverse(level[e] + col, width[:, 0:1])
            cols[3 * e, lanes] = real
            cols[3 * e + 1, lanes] = imag
            cols[3 * e + 2, lanes] = level[e] + col
    rows[4:8, :] = jnp.broadcast_to(width[:, 0:1], (4, B))


def write_pair(pair, slot, shift, mode, direct, swapped, direct_low, swapped_low):
    second = lax.axis_index("energy") % 2 == 1
    is_odd = shift == 2 * mode + 1

    def put(e, first, other):
        for c in range(2):
            pair[slot, e, c] = (first[c].astype(F32) + other[c].astype(F32)).astype(BF16)

    @pl.when(jnp.logical_not(is_odd))
    def _():
        for e in range(2):
            put(e, direct.at[e], swapped.at[e])

    if direct_low is not None:

        @pl.when(jnp.logical_and(is_odd, jnp.logical_not(second)))
        def _():
            put(0, direct.at[1], swapped_low.at[1])
            put(1, direct_low.at[0], swapped.at[0])

        @pl.when(jnp.logical_and(is_odd, second))
        def _():
            put(0, swapped.at[1], direct_low.at[1])
            put(1, swapped_low.at[0], direct.at[0])


def sigma_low_kernel(shift, cells, own, d1, w1, d2, w2, coupling, base, out, pair):
    write_pair(pair, 0, shift[0], 0, d1, w1, own, own)
    write_pair(pair, 1, shift[1], 1, d2, w2, d1, w1)
    weight = cells[0].astype(F32) / MAXCELL
    for e in range(2):
        for c in range(2):
            total = None
            for k in range(2):
                half = mm(coupling[k], pair[k, e, c]).astype(BF16)
                term = mm_nt(half, coupling[k])
                total = term if total is None else total + term
            out[e, c] = base[e, c] + weight * total


def send_faces(e, w_real, w_imag, mats, self0, send_e, send_o, odd):
    right = [mm(mm(mats[0, 0:F], w[128:256, 128:256]).astype(BF16), mats[1]) for w in (w_real, w_imag)]
    left = [mm(mm(mats[2, 0:F], w[0:128, 0:128]).astype(BF16), mats[3]) for w in (w_real, w_imag)]
    to_right = right[0] + pltpu.roll(right[1], F, 1) + self0[e, 0]
    to_left = left[0] + pltpu.roll(left[1], F, 1) + self0[e, 1]
    send_e[e] = pick(odd, to_right, to_left).astype(BF16)
    send_o[e] = pick(odd, to_left, to_right).astype(BF16)


def twice(column):
    return jnp.concatenate((column, column), 1)


def first_kernel(cells, d3, w3, coupling, low, rows, cols, mats, self0, n0, w1, send_e, send_o):
    odd = lax.axis_index("slab") % 2 == 1
    weight = cells[0].astype(F32) / MAXCELL
    for e in range(2):
        n = []
        for c in range(2):
            pair = (d3[e, c].astype(F32) + w3[e, c].astype(F32)).astype(BF16)
            half = mm(coupling[2], pair).astype(BF16)
            value = low[e, c] + weight * mm_nt(half, coupling[2])
            n0[e, c] = value
            n.append(value)
        xr, xi = rows[2 * e : 2 * e + 1], rows[2 * e + 1 : 2 * e + 2]
        tr = damping * (n[0] * xr - n[1] * xi)
        ti = damping * (n[0] * xi + n[1] * xr)
        cr, ci = twice(cols[3 * e]), twice(cols[3 * e + 1])
        wr = cr * tr - ci * ti
        wi = cr * ti + ci * tr
        w1[e, 0] = wr
        w1[e, 1] = wi
        send_faces(e, wr.astype(BF16), wi.astype(BF16), mats, self0, send_e, send_o, odd)


def step_kernel(last, n0, w, rows, cols, out):
    for e in range(2):
        xr, xi = rows[2 * e : 2 * e + 1], rows[2 * e + 1 : 2 * e + 2]
        cr, ci = twice(cols[3 * e]), twice(cols[3 * e + 1])
        nr, ni, wr, wi = n0[e, 0], n0[e, 1], w[e, 0], w[e, 1]
        pr = nr * xr - ni * xi
        pi = nr * xi + ni * xr
        n_split = (halves(nr), halves(ni))
        w_split = (halves(wr), halves(wi))
        rr, ri = complex_mm(n_split, w_split)
        if last:
            dr, di = twice(cols[3 * e + 2]), rows[4:5]
            rr = rr + (pr - (dr * wr - di * wi))
            ri = ri + (pi - (dr * wi + di * wr))
        else:
            rr = rr + 0.25 * pr
            ri = ri + 0.25 * pi
        yr, yi = complex_mm(w_split, (halves(rr), halves(ri)))
        out[e, 0] = wr + damping * (cr * rr - ci * ri + yr)
        out[e, 1] = wi + damping * (cr * ri + ci * rr + yi)


def face_rows(part, w, rows, e):
    at = slice(0, F) if part == 0 else slice(B - F, B)
    index = lax.broadcasted_iota(jnp.int32, (F, B), 0) + (0 if part == 0 else B - F)
    here = lax.broadcasted_iota(jnp.int32, (F, B), 1) == index
    real = w[e, 0, at] + jnp.where(here, rows[2 * e : 2 * e + 1], 0.0)
    imag = w[e, 1, at] + jnp.where(here, rows[2 * e + 1 : 2 * e + 2], 0.0)
    return real, imag


def add_faces(e, recv, packed0, w, done, rows, cols, change):
    scaled = []
    for part, at in ((0, slice(0, F)), (1, slice(B - F, B))):
        delta = (recv[part].astype(F32) - packed0[e, part]).astype(BF16)
        real, imag = face_rows(part, w, rows, e)
        rr = mm(delta, jnp.concatenate((real, -imag), 0).astype(BF16))
        ri = mm(delta, jnp.concatenate((imag, real), 0).astype(BF16))
        change[0, at] = rr.astype(BF16)
        change[1, at] = ri.astype(BF16)
        cr, ci = twice(cols[3 * e, at]), twice(cols[3 * e + 1, at])
        scaled.append((damping * (cr * rr - ci * ri), damping * (cr * ri + ci * rr)))
    wr, wi = w[e, 0].astype(BF16), w[e, 1].astype(BF16)
    qr, qi = change[0], change[1]
    yr = done[e, 0] + damping * (mm(wr, qr) - mm(wi, qi))
    yi = done[e, 1] + damping * (mm(wr, qi) + mm(wi, qr))
    zero = jnp.zeros((B - 2 * F, B), F32)
    yr = yr + jnp.concatenate((scaled[0][0], zero, scaled[1][0]), 0)
    yi = yi + jnp.concatenate((scaled[0][1], zero, scaled[1][1]), 0)
    return yr, yi


def clear(change):
    change[...] = jnp.zeros_like(change)


def second_kernel(recv_e, recv_o, packed0, w1, done, rows, cols, mats, self0, w2, send_e, send_o, change):
    odd = lax.axis_index("slab") % 2 == 1
    clear(change)
    for e in range(2):
        inner = pick(odd, recv_o[e], recv_e[e])
        outer = pick(odd, recv_e[e], recv_o[e])
        yr, yi = add_faces(e, (inner, outer), packed0, w1, done, rows, cols, change.at[e])
        w2[e, 0] = yr
        w2[e, 1] = yi
        send_faces(e, yr.astype(BF16), yi.astype(BF16), mats, self0, send_e, send_o, odd)


def third_kernel(recv_e, recv_o, packed0, w2, done, rows, cols, out, change):
    odd = lax.axis_index("slab") % 2 == 1
    clear(change)
    for e in range(2):
        inner = pick(odd, recv_o[e], recv_e[e])
        outer = pick(odd, recv_e[e], recv_o[e])
        yr, yi = add_faces(e, (inner, outer), packed0, w2, done, rows, cols, change.at[e])
        index = lax.broadcasted_iota(jnp.int32, (B, B), 0)
        here = lax.broadcasted_iota(jnp.int32, (B, B), 1) == index
        out[e, 0] = yr + jnp.where(here, rows[2 * e : 2 * e + 1], 0.0)
        out[e, 1] = yi + jnp.where(here, rows[2 * e + 1 : 2 * e + 2], 0.0)


def on_device(
    green_old,
    hopping,
    phonon_coupling,
    band_offset,
    interface,
    cell_counts,
    contact_flags,
    phonon_shift,
):
    stops = lax.axis_size("energy")
    slabs = lax.axis_size("slab")
    outer_pairs = [(e, (e + 1) % stops) if e % 2 == 1 else (e, (e - 1) % stops) for e in range(stops)]
    same_core = [(e, (e + 2) % stops) if e % 2 == 0 else (e, (e - 2) % stops) for e in range(stops)]
    partner = [(e, e ^ 1) for e in range(stops)]
    even_pairs = [(s, s ^ 1) for s in range(slabs)]
    odd_pairs = [(s, ((s + 1) ^ 1) - 1) for s in range(1, slabs - 1)]

    def move(value, pairs):
        return lax.ppermute(value, "energy", pairs)

    def exchange(to_even, to_odd):
        return lax.ppermute(to_even, "slab", even_pairs), lax.ppermute(to_odd, "slab", odd_pairs)

    own = green_old[:, 0]
    coupling = phonon_coupling[0]
    full = ((2, 2, B, B), F32)
    faces = ((2, F, 128), BF16)
    packs = ((2, 2, F, 128), F32)

    d1 = move(own, outer_pairs)
    w1 = move(own, partner)
    (pack,) = call(pack_kernel, [((72, 128), F32)], 1, 2, 1 << 10)(
        contact_flags, interface[0], band_offset
    )
    near, pack, _ = lax.optimization_barrier((own, pack, w1))
    d2 = move(near, same_core)
    pack_e, pack_o = exchange(pack, pack)
    d3 = move(d1, same_core)
    w2 = move(d1, partner)
    w3 = move(d2, partner)
    base, packed0, self0, rows, cols, mats = call(
        prepare_kernel,
        [full, packs, packs, ((8, B), F32), ((6, B, 128), F32), ((4, 128, 128), BF16)],
        0,
        4,
        1 << 20,
    )(hopping[0], pack, pack_e, pack_o)
    (low,) = call(
        sigma_low_kernel,
        [full],
        2,
        7,
        32 << 24,
        scratch=[pltpu.VMEM((2, 2, 2, B, B), BF16)],
    )(phonon_shift, cell_counts, own, d1, w1, d2, w2, coupling, base)
    n0, x1, send_e, send_o = call(first_kernel, [full, full, faces, faces], 1, 8, 16 << 24)(
        cell_counts, d3, w3, coupling, low, rows, cols, mats, self0
    )
    recv_e, recv_o = exchange(send_e, send_o)
    (done,) = call(lambda *refs: step_kernel(False, *refs), [full], 0, 4, 96 << 24)(n0, x1, rows, cols)
    change = [pltpu.VMEM((2, 2, B, B), BF16)]
    x2, send_e, send_o = call(second_kernel, [full, faces, faces], 0, 9, 16 << 24, scratch=change)(
        recv_e, recv_o, packed0, x1, done, rows, cols, mats, self0
    )
    recv_e, recv_o = exchange(send_e, send_o)
    (done,) = call(lambda *refs: step_kernel(True, *refs), [full], 0, 4, 96 << 24)(n0, x2, rows, cols)
    (out,) = call(third_kernel, [full], 0, 7, 16 << 24, scratch=change)(
        recv_e, recv_o, packed0, x2, done, rows, cols
    )
    return out[:, None]


def solution(mesh):
    placed = (
        P("energy", "slab", None, None, None),
        P("slab", None, None),
        P("slab", None, None, None),
        P("slab", None),
        P("slab", None, None),
        P("slab"),
        P("slab"),
        P(),
    )
    return jax.shard_map(
        on_device,
        mesh=mesh,
        in_specs=placed,
        out_specs=P("energy", "slab", None, None, None),
        check_vma=False,
    )
```
